32 devices in a mesh: groups: 2 (over x), row: 4 (over y, core), col: 4 (over z).
Axes of the slice: x: 2, y: 2, z: 4, core: 2. Of those that a mesh axis runs over, the one named last changes fastest.
Arguments:
- pair_act: bfloat16 [1536, 768, 128], P(('groups', 'row'), 'col'), parts along dimension 0, may hold values from -6 to 6
- ln_gain: float32 [128], replicated, may hold values from 0.1 to 1.9
- ln_bias: float32 [128], replicated, may hold values from -3 to 3
- w_proj: bfloat16 [128, 512], replicated, may hold values from -0.5 to 0.5
- w_gate: bfloat16 [128, 128], replicated, may hold values from -0.5 to 0.5
- out_gain: float32 [128], replicated, may hold values from 0.1 to 1.9
- out_bias: float32 [128], replicated, may hold values from -3 to 3
- w_out: bfloat16 [128, 128], replicated, may hold values from -0.5 to 0.5
Outputs:
- update: bfloat16 [1536, 768, 128], P(('groups', 'row'), 'col'), parts along dimension 0
The draws below stay inside these ranges and needn't reach their ends.
There are 2 independent parts, one for each index of `groups`. The reference program is written for one: setup_inputs(seed, part) draws one part's arguments, and reference() takes and returns one part's arrays. A program takes and returns all parts, laid end to end along the dimension named above; an argument that names none is the same for every part. Nothing has to cross between parts.
All inputs are finite; a program needn't handle non-finite values.
Results may differ from the reference program's by a relative error of at most 0.013.
Values may be sent and summed in bfloat16 or wider, within the bound.
A program may use at most 192 MiB of HBM per device.

```python
import jax
import jax.numpy as jnp
from jax import lax

PAIR_CH = 128
HIDDEN_CH = 128
TOKENS = 768
N_COL = 4


def level_of(own_key, extent, shards, low, high):
    factor_of, own = 1.0, jax.random.fold_in(own_key, 6)
    for dim, parts in shards:
        steps = jnp.exp(jax.random.uniform(jax.random.fold_in(own, dim), (parts,), jnp.float32, low / len(shards), high / len(shards)))
        factor_of = factor_of * jnp.repeat(steps, extent[dim] // parts).reshape([-1 if axis == dim else 1 for axis in range(len(extent))])
    return factor_of


def bell_draw(own_key, shape, width, most, cuts=(), held_as=jnp.bfloat16):
    entries = width * jax.random.normal(own_key, shape, jnp.float32)
    if cuts:
        entries = entries * level_of(own_key, shape, cuts, -0.22, 0.18)
    return jnp.clip(entries, -most, most).astype(held_as)


def setup_inputs(seed: int = 0, part: int = 0) -> dict:
    key_list = jax.random.split(jax.random.key(seed), 9)
    own_keys = jax.random.split(jax.random.fold_in(key_list[8], part), 9)
    pair_act = bell_draw(own_keys[0], (TOKENS, TOKENS, PAIR_CH), 1.0, 6.0, ((0, 4), (1, 4)))
    ln_gain = jnp.clip(1.0 + 0.18 * jax.random.normal(key_list[1], (PAIR_CH,), jnp.float32), 0.1, 1.9)
    ln_bias = bell_draw(key_list[2], (PAIR_CH,), 0.5, 3.0, (), jnp.float32)
    w_proj = bell_draw(key_list[3], (PAIR_CH, 4 * HIDDEN_CH), PAIR_CH ** -0.5, 0.5)
    w_gate = bell_draw(key_list[4], (PAIR_CH, PAIR_CH), PAIR_CH ** -0.5, 0.5)
    out_gain = jnp.clip(1.0 + 0.18 * jax.random.normal(key_list[5], (HIDDEN_CH,), jnp.float32), 0.1, 1.9)
    out_bias = bell_draw(key_list[6], (HIDDEN_CH,), 0.5, 3.0, (), jnp.float32)
    w_out = bell_draw(key_list[7], (HIDDEN_CH, PAIR_CH), HIDDEN_CH ** -0.5, 0.5)
    return {"pair_act": pair_act, "ln_gain": ln_gain, "ln_bias": ln_bias, "w_proj": w_proj, "w_gate": w_gate, "out_gain": out_gain, "out_bias": out_bias, "w_out": w_out}


def layer_norm(values, scale_gain, shift_bias):
    average = lax.optimization_barrier(jnp.mean(values, axis=-1, keepdims=True))
    centred = values - average
    variance = lax.optimization_barrier(jnp.mean(centred * centred, axis=-1, keepdims=True))
    return centred * lax.rsqrt(variance + 1e-05) * scale_gain + shift_bias

def reference(pair_act, ln_gain, ln_bias, w_proj, w_gate, out_gain, out_bias, w_out):
    hidden_width = HIDDEN_CH
    normed = layer_norm(pair_act.astype(jnp.float32), ln_gain, ln_bias).astype(jnp.bfloat16)
    flattened = normed.reshape(TOKENS * TOKENS, PAIR_CH)
    projected = jnp.dot(flattened, w_proj, preferred_element_type=jnp.float32)
    left_side = (jax.nn.sigmoid(projected[:, :hidden_width]) * projected[:, hidden_width:2 * hidden_width]).astype(jnp.bfloat16)
    right_side = (jax.nn.sigmoid(projected[:, 2 * hidden_width:3 * hidden_width]) * projected[:, 3 * hidden_width:]).astype(jnp.bfloat16)
    left_side = left_side.reshape(TOKENS, TOKENS, hidden_width)
    right_side = right_side.reshape(TOKENS, TOKENS, hidden_width)
    gating = jax.nn.sigmoid(jnp.dot(flattened, w_gate, preferred_element_type=jnp.float32)).astype(jnp.bfloat16)
    gating = gating.reshape(TOKENS, TOKENS, PAIR_CH)
    block_size = TOKENS // N_COL

    def add_block(block_index, running):
        first_col = (block_index * block_size).astype(jnp.int32)
        left_block = lax.dynamic_slice_in_dim(left_side, first_col, block_size, 1).astype(jnp.float32)
        right_block = lax.dynamic_slice_in_dim(right_side, first_col, block_size, 1).astype(jnp.float32)
        partial_sum = jnp.einsum('ikh,jkh->ijh', left_block, right_block)
        partial_sum = lax.optimization_barrier(partial_sum.astype(jnp.bfloat16)).astype(jnp.float32)
        return running + partial_sum
    tri_sum = lax.fori_loop(0, N_COL, add_block, jnp.zeros((TOKENS, TOKENS, hidden_width), jnp.float32))
    out_normed = layer_norm(tri_sum, out_gain, out_bias).astype(jnp.bfloat16)
    result = jnp.dot(out_normed.reshape(TOKENS * TOKENS, hidden_width), w_out, preferred_element_type=jnp.float32)
    result = result.reshape(TOKENS, TOKENS, PAIR_CH)
    return (result * gating.astype(jnp.float32)).astype(jnp.bfloat16)
```

```python
import jax
import jax.numpy as jnp
from jax import lax
from jax.sharding import PartitionSpec as P


def layer_norm(values, scale_gain, shift_bias):
    average = jnp.mean(values, axis=-1, keepdims=True)
    centred = values - average
    variance = jnp.mean(centred * centred, axis=-1, keepdims=True)
    return centred * lax.rsqrt(variance + 1e-05) * scale_gain + shift_bias


def gather_rows(block, count):
    if count & (count - 1):
        return lax.all_gather(block, "row", axis=0)
    me = lax.axis_index("row")
    shape = block.shape
    held, bit, depth = block, count // 2, 0
    while bit:
        other = lax.ppermute(held, "row", [(r, r ^ bit) for r in range(count)])
        low = (me & bit) == 0
        held = jnp.stack(
            [jnp.where(low, held, other), jnp.where(low, other, held)], axis=depth
        )
        bit, depth = bit // 2, depth + 1
    return held.reshape((count,) + shape)


def on_device(row_count, chunks, pair_act, ln_gain, ln_bias, w_proj, w_gate, out_gain, out_bias, w_out):
    tile_rows, tile_cols, channels = pair_act.shape
    hidden_width = w_proj.shape[1] // 4

    def glu(flat, first):
        both = jnp.dot(
            flat,
            w_proj[:, first * hidden_width : (first + 2) * hidden_width],
            preferred_element_type=jnp.float32,
        )
        return (jax.nn.sigmoid(both[:, :hidden_width]) * both[:, hidden_width:]).astype(jnp.bfloat16)

    normed = layer_norm(pair_act.astype(jnp.float32), ln_gain, ln_bias).astype(jnp.bfloat16)
    flattened = normed.reshape(tile_rows * tile_cols, channels)
    right_side = glu(flattened, 2).reshape(tile_rows, tile_cols, hidden_width)
    left_side = glu(flattened, 0).reshape(tile_rows, tile_cols, hidden_width)
    gating = (
        jax.nn.sigmoid(jnp.dot(flattened, w_gate, preferred_element_type=jnp.float32))
        .astype(jnp.bfloat16)
        .reshape(tile_rows, tile_cols, channels)
    )
    step = tile_cols // chunks
    pieces = []
    for q in range(chunks):
        gathered = gather_rows(right_side[q * step : (q + 1) * step], row_count)
        partial_sum = jnp.einsum(
            "jkh,ikh->jih",
            gathered.reshape(row_count * step, tile_cols, hidden_width),
            left_side,
            preferred_element_type=jnp.float32,
        )
        tri_sum = lax.psum_scatter(
            partial_sum.astype(jnp.bfloat16), "col", scatter_dimension=0, tiled=True
        ).astype(jnp.float32)
        out_normed = layer_norm(tri_sum, out_gain, out_bias).astype(jnp.bfloat16)
        result = jnp.dot(
            out_normed.reshape(step * tile_rows, hidden_width),
            w_out,
            preferred_element_type=jnp.float32,
        )
        result = jnp.swapaxes(result.reshape(step, tile_rows, channels), 0, 1)
        gate = gating[:, q * step : (q + 1) * step].astype(jnp.float32)
        pieces.append((result * gate).astype(jnp.bfloat16))
    return jnp.concatenate(pieces, axis=1)


def whole_rows(pair_act, ln_gain, ln_bias, w_proj, w_gate, out_gain, out_bias, w_out):
    tile_rows, tile_cols, channels = pair_act.shape
    hidden_width = w_proj.shape[1] // 4
    normed = layer_norm(pair_act.astype(jnp.float32), ln_gain, ln_bias).astype(jnp.bfloat16)
    flattened = normed.reshape(tile_rows * tile_cols, channels)
    projected = jnp.dot(flattened, w_proj, preferred_element_type=jnp.float32)
    left_side = (
        jax.nn.sigmoid(projected[:, :hidden_width]) * projected[:, hidden_width : 2 * hidden_width]
    ).astype(jnp.bfloat16)
    right_side = (
        jax.nn.sigmoid(projected[:, 2 * hidden_width : 3 * hidden_width])
        * projected[:, 3 * hidden_width :]
    ).astype(jnp.bfloat16)
    left_side = left_side.reshape(tile_rows, tile_cols, hidden_width)
    right_side = right_side.reshape(tile_rows, tile_cols, hidden_width)
    gated = jax.nn.sigmoid(jnp.dot(flattened, w_gate, preferred_element_type=jnp.float32)).astype(
        jnp.bfloat16
    )
    gating = gated.reshape(tile_rows, tile_cols, channels)
    partial_sum = jnp.einsum(
        "jkh,ikh->jih",
        lax.all_gather(right_side, "row", axis=0, tiled=True),
        left_side,
        preferred_element_type=jnp.float32,
    )
    tri_sum = lax.psum_scatter(
        partial_sum.astype(jnp.bfloat16), "col", scatter_dimension=0, tiled=True
    ).astype(jnp.float32)
    out_normed = layer_norm(tri_sum, out_gain, out_bias).astype(jnp.bfloat16)
    result = jnp.dot(
        out_normed.reshape(tile_cols * tile_rows, hidden_width),
        w_out,
        preferred_element_type=jnp.float32,
    )
    result = jnp.swapaxes(result.reshape(tile_cols, tile_rows, channels), 0, 1)
    return (result * gating.astype(jnp.float32)).astype(jnp.bfloat16)


def solution(mesh):
    rows, cols = mesh.shape["row"], mesh.shape["col"]

    def body(pair_act, *params):
        tile_rows, tile_cols, _ = pair_act.shape
        chunks = 4 if tile_rows == tile_cols and rows == cols and tile_cols % 32 == 0 else 0
        if chunks:
            return on_device(rows, chunks, pair_act, *params)
        return whole_rows(pair_act, *params)

    whole = P(None, None)
    return jax.shard_map(
        body,
        mesh=mesh,
        in_specs=(
            P(("groups", "row"), "col", None), P(None), P(None), whole, whole, P(None), P(None), whole,
        ),
        out_specs=P(("groups", "row"), "col", None),
        check_vma=False,
    )
```
